32 devices in a mesh: row: 8 (over z, y), col: 4 (over x, core).
Axes of the slice: x: 2, y: 2, z: 4, core: 2. Of those that a mesh axis runs over, the one named last changes fastest.
Arguments:
- nodes_zero: float32 [8192, 64], P('row'), may hold values from -28 to 28
- nodes_one: float32 [8192, 64], P(('row', 'col')), may hold values from -28 to 28
- nodes_two: float32 [8192, 64], P('col'), may hold values from -28 to 28
- precision: float32 [64], replicated, may hold values from 0.1 to 0.4
- drift: float32 [64], replicated, may hold values from -1.2 to 1.2
- terminal: bfloat16 [8192, 128], P('col'), may hold values from -6 to 6
- exercise_one: float32 [8192, 128], P(('row', 'col')), may hold values from -6 to 6
- exercise_zero: float32 [8192, 128], P(('row', 'col')), may hold values from -6 to 6
- exercise_flags: int32 [2, 128], replicated, may hold values 0 or 1
Outputs:
- value_one: float32 [8192, 128], P(('row', 'col'))
- value_zero: float32 [8192, 128], P(('row', 'col'))
The draws below stay inside these ranges and needn't reach their ends.
All inputs are finite; a program needn't handle non-finite values.
Results may differ from the reference program's by a relative error of at most 0.0012.
Values may be sent and summed in bfloat16 or wider, within the bound.
A program may use at most 64 MiB of HBM per device.

```python
import math
import jax
import jax.numpy as jnp
from jax import lax

D = 64
TRADES = 128
SRC_DEV = 1024
NODES = 8192


def node_draw(key, date):
    own = jax.random.fold_in(key, 17 + date)
    drawn = jax.random.truncated_normal(own, -6.0, 6.0, (NODES, D), jnp.float32)
    if date == 0:
        return drawn
    direction = 1.0 if date == 2 else -1.0
    places = jax.random.randint(jax.random.fold_in(own, 5), (4,), 8, NODES).astype(jnp.int32)
    remote = direction * jax.random.uniform(jax.random.fold_in(own, 7), (4, D), jnp.float32, 26.0, 28.0)
    return drawn.at[places].set(remote)


def draw_nodes_zero(key, part):
    return node_draw(key, 0)


def draw_nodes_one(key, part):
    return node_draw(key, 1)


def draw_nodes_two(key, part):
    return node_draw(key, 2)


def set_ends(values, rng, least, high):
    longest = values.shape.index(max(values.shape))
    spots = []
    for shift in (0, 1):
        where = [jax.random.randint(jax.random.fold_in(rng, axis), (), 0, length) for axis, length in enumerate(values.shape)]
        where[longest] = (where[longest] + shift) % values.shape[longest]
        spots.append(tuple(where))
    return values.at[spots[0]].set(least).at[spots[1]].set(high)


def levels(own_key, shape, cuts, smallest, top_value):
    factor_of = 1.0
    for dim, parts in cuts:
        heights = jax.random.uniform(jax.random.fold_in(jax.random.fold_in(own_key, 6), dim), (parts,), jnp.float32, smallest / len(cuts), top_value / len(cuts))
        factor_of = factor_of * jnp.repeat(jnp.exp(heights), shape[dim] // parts).reshape((-1,) + (1,) * (len(shape) - 1 - dim))
    return factor_of


def scatter_about(rng, dims, deviation, most, cuts=(), kind=jnp.bfloat16):
    values = deviation * jax.random.normal(rng, dims, jnp.float32)
    if cuts:
        values = values * levels(rng, dims, cuts, -0.22, 0.18)
    return jnp.clip(values, -most, most).astype(kind)


def setup_inputs(seed: int = 0) -> dict:
    seeds = jax.random.split(jax.random.key(seed), 10)
    nodes_zero = draw_nodes_zero(jax.random.fold_in(seeds[9], 71), 0)
    nodes_one = draw_nodes_one(jax.random.fold_in(seeds[9], 71), 0)
    nodes_two = draw_nodes_two(jax.random.fold_in(seeds[9], 71), 0)
    precision = jnp.clip(jnp.exp(jax.random.uniform(seeds[3], (D,), jnp.float32, math.log(0.1), math.log(0.4))), 0.1, 0.4)
    drift = scatter_about(seeds[4], (D,), 0.3, 1.2, (), jnp.float32)
    terminal = scatter_about(seeds[5], (NODES, TRADES), 1.0, 6.0, ((0, 4),))
    exercise_one = scatter_about(seeds[6], (NODES, TRADES), 1.0, 6.0, ((0, 32),), jnp.float32)
    exercise_zero = scatter_about(seeds[7], (NODES, TRADES), 1.0, 6.0, ((0, 32),), jnp.float32)
    exercise_flags = set_ends((jax.random.randint(seeds[8], (2, TRADES), 0, 2) < 1).astype(jnp.int32), jax.random.fold_in(seeds[8], 1), 0, 1)
    return {"nodes_zero": nodes_zero, "nodes_one": nodes_one, "nodes_two": nodes_two, "precision": precision, "drift": drift, "terminal": terminal, "exercise_one": exercise_one, "exercise_zero": exercise_zero, "exercise_flags": exercise_flags}


def scores_of(queries, offsets, targets):
    product = lax.dot_general(queries, targets, (((1,), (1,)), ((), ())), preferred_element_type=jnp.float32)
    return product - offsets[:, None]


def continuation(sources, targets, prices, precision, drift):
    shifted = sources + drift
    queries = (shifted * precision).astype(jnp.bfloat16)
    offsets = 0.5 * jnp.sum(precision * shifted * shifted, axis=1)
    blocks = sources.shape[0] // SRC_DEV
    query_blocks = queries.reshape(blocks, SRC_DEV, -1)
    offset_blocks = offsets.reshape(blocks, SRC_DEV)

    def gather_stats(state, pieces):
        maxima, totals = state
        scores = scores_of(pieces[0], pieces[1], targets)
        highest = jnp.maximum(maxima, jnp.max(scores, axis=0))
        totals = totals * jnp.exp(maxima - highest) + jnp.sum(jnp.exp(scores - highest[None, :]), axis=0)
        return (highest, totals), None

    start_max = jnp.full((targets.shape[0],), -jnp.inf, jnp.float32)
    start_total = jnp.zeros((targets.shape[0],), jnp.float32)
    (maxima, totals), unused = lax.scan(gather_stats, (start_max, start_total), (query_blocks, offset_blocks))
    inverse = 1.0 / totals

    def carried(pieces):
        scores = scores_of(pieces[0], pieces[1], targets)
        weights = (jnp.exp(scores - maxima[None, :]) * inverse[None, :]).astype(jnp.bfloat16)
        return jnp.dot(weights, prices, preferred_element_type=jnp.float32)

    return lax.map(carried, (query_blocks, offset_blocks)).reshape(sources.shape[0], -1)


def settle(carried, exercise, allowed):
    return jnp.where(allowed[None, :] == 1, jnp.maximum(exercise, carried), carried)


def reference(nodes_zero, nodes_one, nodes_two, precision, drift, terminal, exercise_one, exercise_zero, exercise_flags):
    carry_one = continuation(nodes_one, nodes_two.astype(jnp.bfloat16), terminal, precision, drift)
    value_one = settle(carry_one, exercise_one, exercise_flags[1])
    carry_zero = continuation(nodes_zero, nodes_one.astype(jnp.bfloat16), value_one.astype(jnp.bfloat16), precision, drift)
    value_zero = settle(carry_zero, exercise_zero, exercise_flags[0])
    return value_one, value_zero
```

```python
import functools

import jax
import jax.numpy as jnp
from jax import lax
from jax.experimental import pallas as pl
from jax.experimental.pallas import tpu as pltpu
from jax.sharding import PartitionSpec as P

MESH = pl.DeviceIdType.MESH
TILE = 256


def pieces_of(column, lanes):
    first = column.astype(jnp.bfloat16).astype(jnp.float32)
    rest = column - first
    second = rest.astype(jnp.bfloat16).astype(jnp.float32)
    third = rest - second
    lane = lax.broadcasted_iota(jnp.int32, (column.shape[0], lanes), 1)
    out = jnp.where(lane == 0, first, jnp.where(lane == 1, second, jnp.where(lane == 2, third, 0.0)))
    return out.astype(jnp.bfloat16)


def put_queries(view, nodes, precision, drift):
    depth = nodes.shape[1]
    shifted = nodes + drift
    view[:, :depth] = (shifted * precision).astype(jnp.bfloat16)
    offsets = 0.5 * jnp.sum(precision * shifted * shifted, axis=1, keepdims=True)
    view[:, depth:] = pieces_of(offsets, view.shape[1] - depth)


def put_targets(view, nodes):
    depth = nodes.shape[1]
    view[:, :depth] = nodes.astype(jnp.bfloat16)
    lane = lax.broadcasted_iota(jnp.int32, (nodes.shape[0], view.shape[1] - depth), 1)
    view[:, depth:] = jnp.where(lane < 3, -1.0, 0.0).astype(jnp.bfloat16)


def body(
    rows,
    cols,
    nz_ref,
    n1_ref,
    n2_ref,
    precision_ref,
    drift_ref,
    terminal_ref,
    ex1_ref,
    ex0_ref,
    flags_ref,
    v1_ref,
    v0_ref,
    q1,
    t1,
    q0,
    t2,
    e1,
    e0,
    st1,
    st0,
    f1,
    f0,
    price,
    out1,
    in1,
    out0,
    in0,
    q_send,
    q_recv,
    t_send,
    t_recv,
    s1_send,
    s1_recv,
    s0_send,
    s0_recv,
    p_send,
    p_recv,
    r1_send,
    r1_recv,
    r0_send,
    r0_recv,
):
    r = lax.axis_index("row")
    c = lax.axis_index("col")
    own = n1_ref.shape[0]
    sources = nz_ref.shape[0]
    targets = n2_ref.shape[0]
    chunks, _, width = e1.shape
    precision = precision_ref[...]
    drift = drift_ref[...]

    barrier = pltpu.get_barrier_semaphore()
    for d in range(1, rows):
        pl.semaphore_signal(barrier, inc=1, device_id=(lax.rem(r + d, rows), c), device_id_type=MESH)
    for d in range(1, cols):
        pl.semaphore_signal(barrier, inc=1, device_id=(r, lax.rem(c + d, cols)), device_id_type=MESH)

    put_queries(q1.at[c], n1_ref[...], precision, drift)
    put_targets(t1.at[r], n1_ref[...])
    pl.semaphore_wait(barrier, rows + cols - 2)

    def to_rows(buf, send, recv):
        def make(d, slot):
            return pltpu.make_async_remote_copy(
                src_ref=buf.at[slot],
                dst_ref=buf.at[slot],
                send_sem=send.at[d],
                recv_sem=recv.at[d],
                device_id=(lax.rem(r + d, rows), c),
                device_id_type=MESH,
            )

        return make

    def start_rows(buf, send, recv):
        make = to_rows(buf, send, recv)
        for d in range(1, rows):
            make(d, r).start()

    def recv_rows(buf, send, recv):
        make = to_rows(buf, send, recv)
        for d in range(1, rows):
            make(d, lax.rem(r + rows - d, rows)).wait_recv()

    def sent_rows(buf, send, recv):
        make = to_rows(buf, send, recv)
        for d in range(1, rows):
            make(d, r).wait_send()

    def q_copy(d, slot):
        return pltpu.make_async_remote_copy(
            src_ref=q1.at[slot],
            dst_ref=q1.at[slot],
            send_sem=q_send.at[d],
            recv_sem=q_recv.at[d],
            device_id=(r, lax.rem(c + d, cols)),
            device_id_type=MESH,
        )

    for d in range(1, cols):
        q_copy(d, c).start()
    start_rows(t1, t_send, t_recv)

    put_targets(t2, n2_ref[...])
    put_queries(q0, nz_ref[...], precision, drift)

    step = min(TILE, sources)

    def stats(load_queries, load_targets, e, st, slot):
        def one(k, carry):
            target = load_targets(k)
            peak = None
            for at in range(0, sources, step):
                s = lax.dot_general(
                    load_queries(at), target, (((1,), (1,)), ((), ())), preferred_element_type=jnp.float32
                )
                e[k, at : at + step, :] = s
                top = jnp.max(s.reshape(step // 8, 8, width), axis=0)
                peak = top if peak is None else jnp.maximum(peak, top)
            peak = jnp.max(peak, axis=0, keepdims=True)
            total = jnp.zeros((8, width), jnp.float32)
            for at in range(0, sources, step):
                x = jnp.exp(e[k, at : at + step, :] - peak)
                e[k, at : at + step, :] = x
                total = total + jnp.sum(x.reshape(step // 8, 8, width), axis=0)
            st[slot, 0, pl.ds(k, 1), :] = peak
            st[slot, 1, pl.ds(k, 1), :] = jnp.sum(total, axis=0, keepdims=True)
            return carry

        lax.fori_loop(0, chunks, one, 0)

    def factor(st, f):
        peak = st[0, 0]
        for i in range(1, rows):
            peak = jnp.maximum(peak, st[i, 0])
        total = jnp.zeros_like(peak)
        for i in range(rows):
            total = total + st[i, 1] * jnp.exp(st[i, 0] - peak)
        f[...] = jnp.exp(st[r, 0] - peak) * (1.0 / total)

    for d in range(1, cols):
        q_copy(d, lax.rem(c + cols - d, cols)).wait_recv()

    def q1_rows(at):
        return q1[at // own : (at + step) // own].reshape(step, q1.shape[2])

    stats(q1_rows, lambda k: t2[pl.ds(k * width, width), :], e1, st1, r)
    start_rows(st1, s1_send, s1_recv)

    recv_rows(t1, t_send, t_recv)
    per = width // own

    def t1_rows(k):
        return t1[pl.ds(k * per, per)].reshape(width, t1.shape[2])

    stats(lambda at: q0[at : at + step, :], t1_rows, e0, st0, r)
    start_rows(st0, s0_send, s0_recv)

    recv_rows(st1, s1_send, s1_recv)
    factor(st1, f1)

    def partial_of(e, f, load_prices, block):
        def one(k, total):
            w = (e[k, pl.ds(block * own, own), :] * f[pl.ds(k, 1), :]).astype(jnp.bfloat16)
            return total + jnp.dot(w, load_prices(k), preferred_element_type=jnp.float32)

        return lax.fori_loop(0, chunks, one, jnp.zeros((own, v1_ref.shape[1]), jnp.float32))

    def reduce(e, f, load_prices, out, into, send, recv):
        def make(d):
            return pltpu.make_async_remote_copy(
                src_ref=out.at[d],
                dst_ref=into.at[d],
                send_sem=send.at[d],
                recv_sem=recv.at[d],
                device_id=(r, lax.rem(c + d, cols)),
                device_id_type=MESH,
            )

        for d in range(1, cols):
            out[d] = partial_of(e, f, load_prices, lax.rem(c + d, cols))
            make(d).start()
        total = partial_of(e, f, load_prices, c)
        for d in range(1, cols):
            make(d).wait_recv()
            total = total + into[d]
        return total, lambda: [make(d).wait_send() for d in range(1, cols)]

    carried, done1 = reduce(
        e1, f1, lambda k: terminal_ref[pl.ds(k * width, width), :], out1, in1, r1_send, r1_recv
    )
    value = jnp.where(flags_ref[1:2, :] == 1, jnp.maximum(ex1_ref[...], carried), carried)
    v1_ref[...] = value
    price[r] = value.astype(jnp.bfloat16)
    start_rows(price, p_send, p_recv)

    recv_rows(st0, s0_send, s0_recv)
    factor(st0, f0)
    recv_rows(price, p_send, p_recv)

    def price_rows(k):
        return price[pl.ds(k * per, per)].reshape(width, price.shape[2])

    carried, done0 = reduce(e0, f0, price_rows, out0, in0, r0_send, r0_recv)
    v0_ref[...] = jnp.where(flags_ref[0:1, :] == 1, jnp.maximum(ex0_ref[...], carried), carried)

    for d in range(1, cols):
        q_copy(d, c).wait_send()
    sent_rows(t1, t_send, t_recv)
    sent_rows(st1, s1_send, s1_recv)
    sent_rows(st0, s0_send, s0_recv)
    sent_rows(price, p_send, p_recv)
    done1()
    done0()


def shards(rows, cols, nodes_zero, nodes_one, nodes_two, precision, drift, terminal, ex1, ex0, flags):
    own, depth = nodes_one.shape
    sources = nodes_zero.shape[0]
    targets = nodes_two.shape[0]
    trades = terminal.shape[1]
    width = max(own, min(TILE, targets))
    chunks = targets // width
    lanes = 128 * (-(-(depth + 3) // 128))
    dma = pltpu.SemaphoreType.DMA
    vmem = pl.BlockSpec(memory_space=pltpu.VMEM)
    out = jax.ShapeDtypeStruct((own, trades), jnp.float32)
    stat = pltpu.VMEM((rows, 2, chunks, width), jnp.float32)
    tall = pltpu.VMEM((chunks, sources, width), jnp.float32)
    few = pltpu.VMEM((chunks, width), jnp.float32)
    parts = pltpu.VMEM((cols, own, trades), jnp.float32)
    return pl.pallas_call(
        functools.partial(body, rows, cols),
        out_shape=(out, out),
        in_specs=[vmem] * 9,
        out_specs=(vmem, vmem),
        scratch_shapes=[
            pltpu.VMEM((cols, own, lanes), jnp.bfloat16),
            pltpu.VMEM((rows, own, lanes), jnp.bfloat16),
            pltpu.VMEM((sources, lanes), jnp.bfloat16),
            pltpu.VMEM((targets, lanes), jnp.bfloat16),
            tall,
            tall,
            stat,
            stat,
            few,
            few,
            pltpu.VMEM((rows, own, trades), jnp.bfloat16),
            parts,
            parts,
            parts,
            parts,
            dma((cols,)),
            dma((cols,)),
            dma((rows,)),
            dma((rows,)),
            dma((rows,)),
            dma((rows,)),
            dma((rows,)),
            dma((rows,)),
            dma((rows,)),
            dma((rows,)),
            dma((cols,)),
            dma((cols,)),
            dma((cols,)),
            dma((cols,)),
        ],
        compiler_params=pltpu.CompilerParams(
            collective_id=0, has_side_effects=True, vmem_limit_bytes=56 * 1024 * 1024
        ),
    )(nodes_zero, nodes_one, nodes_two, precision[None, :], drift[None, :], terminal, ex1, ex0, flags)


def solution(mesh):
    both = P(("row", "col"), None)
    return jax.shard_map(
        functools.partial(shards, mesh.shape["row"], mesh.shape["col"]),
        mesh=mesh,
        in_specs=(P("row", None), both, P("col", None), P(), P(), P("col", None), both, both, P()),
        out_specs=(both, both),
        check_vma=False,
    )
```

```python
import functools

import jax
import jax.numpy as jnp
from jax import lax
from jax.experimental import pallas as pl
from jax.experimental.pallas import tpu as pltpu
from jax.sharding import PartitionSpec as P

MESH = pl.DeviceIdType.MESH
TILE = 256


def column_of(row):
    return jnp.broadcast_to(row, (128, row.shape[1])).T[:, :1]


def queries_of(nodes, precision, drift, height):
    shifted = nodes + drift
    offsets = 0.5 * jnp.sum(precision * shifted * shifted, axis=0, keepdims=True)
    first = offsets.astype(jnp.bfloat16).astype(jnp.float32)
    rest = offsets - first
    second = rest.astype(jnp.bfloat16).astype(jnp.float32)
    third = rest - second
    count = height - nodes.shape[0]
    at = lax.broadcasted_iota(jnp.int32, (count, nodes.shape[1]), 0)
    extra = jnp.where(at == 0, first, jnp.where(at == 1, second, jnp.where(at == 2, third, 0.0)))
    return jnp.concatenate([shifted * precision, extra], axis=0)


def upright(tall, lanes):
    short = lanes - tall.shape[0]
    if short:
        tall = jnp.concatenate([tall, jnp.zeros((short, tall.shape[1]), tall.dtype)], axis=0)
    return tall.T.astype(jnp.bfloat16)


def ones_under(count, width):
    at = lax.broadcasted_iota(jnp.int32, (count, width), 0)
    return jnp.where(at < 3, -1.0, 0.0).astype(jnp.bfloat16)


def body(
    rows,
    cols,
    nz_ref,
    n1_ref,
    n2_ref,
    precision_ref,
    drift_ref,
    terminal_ref,
    ex1_ref,
    ex0_ref,
    flags_ref,
    v1_ref,
    v0_ref,
    q1t,
    q1,
    t1,
    q0,
    t2,
    e1,
    e0,
    w0,
    st1,
    st0,
    f1,
    f0,
    price,
    out1,
    in1,
    out0,
    in0,
    q_send,
    q_recv,
    t_send,
    t_recv,
    s1_send,
    s1_recv,
    s0_send,
    s0_recv,
    p_send,
    p_recv,
    r1_send,
    r1_recv,
    r0_send,
    r0_recv,
):
    r = lax.axis_index("row")
    c = lax.axis_index("col")
    depth, own = n1_ref.shape
    sources = nz_ref.shape[1]
    lanes = q0.shape[1]
    height = q1t.shape[1]
    chunks, _, width = e1.shape
    precision = column_of(precision_ref[...])
    drift = column_of(drift_ref[...])

    barrier = pltpu.get_barrier_semaphore()
    for d in range(1, rows):
        pl.semaphore_signal(barrier, inc=1, device_id=(lax.rem(r + d, rows), c), device_id_type=MESH)
    for d in range(1, cols):
        pl.semaphore_signal(barrier, inc=1, device_id=(r, lax.rem(c + d, cols)), device_id_type=MESH)

    mine = queries_of(n1_ref[...], precision, drift, height)
    q1t[c] = mine.astype(jnp.bfloat16)
    t1[r, :depth, :] = n1_ref[...].astype(jnp.bfloat16)
    pl.semaphore_wait(barrier, rows + cols - 2)

    def to_rows(buf, send, recv):
        def make(d, slot):
            view = buf.at[slot, pl.ds(0, depth)] if buf is t1 else buf.at[slot]
            return pltpu.make_async_remote_copy(
                src_ref=view,
                dst_ref=view,
                send_sem=send.at[d],
                recv_sem=recv.at[d],
                device_id=(lax.rem(r + d, rows), c),
                device_id_type=MESH,
            )

        return make

    def start_rows(buf, send, recv):
        make = to_rows(buf, send, recv)
        for d in range(1, rows):
            make(d, r).start()

    def recv_rows(buf, send, recv):
        make = to_rows(buf, send, recv)
        for d in range(1, rows):
            make(d, lax.rem(r + rows - d, rows)).wait_recv()

    def sent_rows(buf, send, recv):
        make = to_rows(buf, send, recv)
        for d in range(1, rows):
            make(d, r).wait_send()

    def q_copy(d, slot):
        return pltpu.make_async_remote_copy(
            src_ref=q1t.at[slot],
            dst_ref=q1t.at[slot],
            send_sem=q_send.at[d],
            recv_sem=q_recv.at[d],
            device_id=(r, lax.rem(c + d, cols)),
            device_id_type=MESH,
        )

    for d in range(1, cols):
        q_copy(d, c).start()
    start_rows(t1, t_send, t_recv)

    for k in range(chunks):
        t2[k, :depth, :] = n2_ref[:, k * width : (k + 1) * width].astype(jnp.bfloat16)
        t2[k, depth:, :] = ones_under(lanes - depth, width)
    q1[c] = upright(mine, lanes)
    q0[...] = upright(queries_of(nz_ref[...], precision, drift, height), lanes)
    for i in range(rows):
        t1[i, depth:, :] = ones_under(lanes - depth, own)

    step = min(TILE, sources)

    def stats(load_queries, load_targets, e, st, begin, end):
        def one(k, carry):
            target = load_targets(k)
            peak = None
            for at in range(0, sources, step):
                s = lax.dot_general(
                    load_queries(at), target, (((1,), (0,)), ((), ())), preferred_element_type=jnp.float32
                )
                e[k, at : at + step, :] = s
                top = jnp.max(s.reshape(step // 8, 8, width), axis=0)
                peak = top if peak is None else jnp.maximum(peak, top)
            peak = jnp.max(peak, axis=0, keepdims=True)
            total = jnp.zeros((8, width), jnp.float32)
            for at in range(0, sources, step):
                x = jnp.exp(e[k, at : at + step, :] - peak)
                e[k, at : at + step, :] = x
                total = total + jnp.sum(x.reshape(step // 8, 8, width), axis=0)
            st[r, 0, pl.ds(k, 1), :] = peak
            st[r, 1, pl.ds(k, 1), :] = jnp.sum(total, axis=0, keepdims=True)
            return carry

        lax.fori_loop(begin, end, one, 0)

    def factor(st, f):
        peak = st[0, 0]
        for i in range(1, rows):
            peak = jnp.maximum(peak, st[i, 0])
        total = jnp.zeros_like(peak)
        for i in range(rows):
            total = total + st[i, 1] * jnp.exp(st[i, 0] - peak)
        f[...] = jnp.exp(st[r, 0] - peak) * (1.0 / total)

    for d in range(1, cols):
        slot = lax.rem(c + cols - d, cols)
        q_copy(d, slot).wait_recv()
        q1[slot] = upright(q1t[slot].astype(jnp.float32), lanes)

    def q1_rows(at):
        return q1[at // own : (at + step) // own].reshape(step, q1.shape[2])

    stats(q1_rows, lambda k: t2[k], e1, st1, 0, chunks)
    start_rows(st1, s1_send, s1_recv)

    recv_rows(t1, t_send, t_recv)
    per = width // own

    def t1_rows(k):
        if per == 1:
            return t1[k]
        return jnp.concatenate([t1[k * per + i] for i in range(per)], axis=1)

    def stats_zero(begin, end):
        stats(lambda at: q0[at : at + step, :], t1_rows, e0, st0, begin, end)

    half = (chunks + 1) // 2
    stats_zero(0, half)

    recv_rows(st1, s1_send, s1_recv)
    factor(st1, f1)

    def partial_of(weights, load_prices, block):
        total = jnp.zeros((own, v1_ref.shape[1]), jnp.float32)
        for k in range(chunks):
            total = total + jnp.dot(weights(k, block), load_prices(k), preferred_element_type=jnp.float32)
        return total

    def reduce(weights, load_prices, out, into, send, recv, between):
        def make(d):
            return pltpu.make_async_remote_copy(
                src_ref=out.at[d],
                dst_ref=into.at[d],
                send_sem=send.at[d],
                recv_sem=recv.at[d],
                device_id=(r, lax.rem(c + d, cols)),
                device_id_type=MESH,
            )

        for d in range(1, cols):
            out[d] = partial_of(weights, load_prices, lax.rem(c + d, cols))
            make(d).start()
        total = partial_of(weights, load_prices, c)
        between()
        for d in range(1, cols):
            make(d).wait_recv()
            total = total + into[d]
        return total, lambda: [make(d).wait_send() for d in range(1, cols)]

    def weights_one(k, block):
        return (e1[k, pl.ds(block * own, own), :] * f1[pl.ds(k, 1), :]).astype(jnp.bfloat16)

    def rest_zero():
        stats_zero(half, chunks)
        start_rows(st0, s0_send, s0_recv)

    carried, done1 = reduce(
        weights_one,
        lambda k: terminal_ref[k * width : (k + 1) * width, :],
        out1,
        in1,
        r1_send,
        r1_recv,
        rest_zero,
    )
    value = jnp.where(flags_ref[1:2, :] == 1, jnp.maximum(ex1_ref[...], carried), carried)
    v1_ref[...] = value
    price[r] = value.astype(jnp.bfloat16)
    partner = r + 1 - 2 * lax.rem(r, 2)
    half_rows = rows // 2

    def along(k, slot):
        return pltpu.make_async_remote_copy(
            src_ref=price.at[slot],
            dst_ref=price.at[slot],
            send_sem=p_send.at[k],
            recv_sem=p_recv.at[k],
            device_id=(lax.rem(r + 2 * k, rows), c),
            device_id_type=MESH,
        )

    def across(k, slot):
        return pltpu.make_async_remote_copy(
            src_ref=price.at[slot],
            dst_ref=price.at[slot],
            send_sem=p_send.at[half_rows + k],
            recv_sem=p_recv.at[half_rows + k],
            device_id=(partner, c),
            device_id_type=MESH,
        )

    across(0, r).start()
    for k in range(1, half_rows):
        along(k, r).start()

    recv_rows(st0, s0_send, s0_recv)
    factor(st0, f0)

    def weigh(k, carry):
        for at in range(0, sources, step):
            w0[k, at : at + step, :] = (e0[k, at : at + step, :] * f0[pl.ds(k, 1), :]).astype(jnp.bfloat16)
        return carry

    share = chunks // max(half_rows - 1, 1)
    for k in range(1, half_rows):
        lax.fori_loop((k - 1) * share, chunks if k == half_rows - 1 else k * share, weigh, 0)
        slot = lax.rem(r + rows - 2 * k, rows)
        along(k, slot).wait_recv()
        across(k, slot).start()
    for k in range(half_rows):
        across(k, lax.rem(partner + rows - 2 * k, rows)).wait_recv()

    def price_rows(k):
        return price[k * per : (k + 1) * per].reshape(width, price.shape[2])

    def weights_zero(k, block):
        return w0[k, pl.ds(block * own, own), :]

    carried, done0 = reduce(weights_zero, price_rows, out0, in0, r0_send, r0_recv, lambda: None)
    v0_ref[...] = jnp.where(flags_ref[0:1, :] == 1, jnp.maximum(ex0_ref[...], carried), carried)

    for d in range(1, cols):
        q_copy(d, c).wait_send()
    sent_rows(t1, t_send, t_recv)
    sent_rows(st1, s1_send, s1_recv)
    sent_rows(st0, s0_send, s0_recv)
    for k in range(half_rows):
        across(k, r).wait_send()
        if k:
            along(k, r).wait_send()
    done1()
    done0()


def shards(rows, cols, nodes_zero, nodes_one, nodes_two, precision, drift, terminal, ex1, ex0, flags):
    own, depth = nodes_one.shape
    height = depth + 16
    sources = nodes_zero.shape[0]
    targets = nodes_two.shape[0]
    trades = terminal.shape[1]
    width = max(own, min(TILE, targets))
    chunks = targets // width
    lanes = 128 * (-(-(depth + 3) // 128))
    dma = pltpu.SemaphoreType.DMA
    vmem = pl.BlockSpec(memory_space=pltpu.VMEM)
    out = jax.ShapeDtypeStruct((own, trades), jnp.float32)
    stat = pltpu.VMEM((rows, 2, chunks, width), jnp.float32)
    tall = pltpu.VMEM((chunks, sources, width), jnp.float32)
    few = pltpu.VMEM((chunks, width), jnp.float32)
    parts = pltpu.VMEM((cols, own, trades), jnp.float32)
    return pl.pallas_call(
        functools.partial(body, rows, cols),
        out_shape=(out, out),
        in_specs=[vmem] * 9,
        out_specs=(vmem, vmem),
        scratch_shapes=[
            pltpu.VMEM((cols, height, own), jnp.bfloat16),
            pltpu.VMEM((cols, own, lanes), jnp.bfloat16),
            pltpu.VMEM((rows, lanes, own), jnp.bfloat16),
            pltpu.VMEM((sources, lanes), jnp.bfloat16),
            pltpu.VMEM((chunks, lanes, width), jnp.bfloat16),
            tall,
            tall,
            pltpu.VMEM((chunks, sources, width), jnp.bfloat16),
            stat,
            stat,
            few,
            few,
            pltpu.VMEM((rows, own, trades), jnp.bfloat16),
            parts,
            parts,
            parts,
            parts,
            dma((cols,)),
            dma((cols,)),
            dma((rows,)),
            dma((rows,)),
            dma((rows,)),
            dma((rows,)),
            dma((rows,)),
            dma((rows,)),
            dma((rows,)),
            dma((rows,)),
            dma((cols,)),
            dma((cols,)),
            dma((cols,)),
            dma((cols,)),
        ],
        compiler_params=pltpu.CompilerParams(
            collective_id=0, has_side_effects=True, vmem_limit_bytes=56 * 1024 * 1024
        ),
    )(nodes_zero.T, nodes_one.T, nodes_two.T, precision[None, :], drift[None, :], terminal, ex1, ex0, flags)


def solution(mesh):
    both = P(("row", "col"), None)
    return jax.shard_map(
        functools.partial(shards, mesh.shape["row"], mesh.shape["col"]),
        mesh=mesh,
        in_specs=(P("row", None), both, P("col", None), P(), P(), P("col", None), both, both, P()),
        out_specs=(both, both),
        check_vma=False,
    )
```

```python
import functools

import jax
import jax.numpy as jnp
from jax import lax
from jax.experimental import pallas as pl
from jax.experimental.pallas import tpu as pltpu
from jax.sharding import PartitionSpec as P

MESH = pl.DeviceIdType.MESH
TILE = 256
PARTS = 2
LIMIT = 62 * 1024 * 1024


def column_of(row):
    return jnp.broadcast_to(row, (128, row.shape[1])).T[:, :1]


def queries_of(nodes, precision, drift, height):
    shifted = nodes + drift
    offsets = 0.5 * jnp.sum(precision * shifted * shifted, axis=0, keepdims=True)
    first = offsets.astype(jnp.bfloat16).astype(jnp.float32)
    rest = offsets - first
    second = rest.astype(jnp.bfloat16).astype(jnp.float32)
    third = rest - second
    count = height - nodes.shape[0]
    at = lax.broadcasted_iota(jnp.int32, (count, nodes.shape[1]), 0)
    extra = jnp.where(at == 0, first, jnp.where(at == 1, second, jnp.where(at == 2, third, 0.0)))
    return jnp.concatenate([shifted * precision, extra], axis=0)


def upright(tall, lanes):
    short = lanes - tall.shape[0]
    if short:
        tall = jnp.concatenate([tall, jnp.zeros((short, tall.shape[1]), tall.dtype)], axis=0)
    return tall.T.astype(jnp.bfloat16)


def ones_under(count, width):
    at = lax.broadcasted_iota(jnp.int32, (count, width), 0)
    return jnp.where(at < 3, -1.0, 0.0).astype(jnp.bfloat16)


def body(
    rows,
    cols,
    nz_hbm,
    n1_hbm,
    n2_hbm,
    precision_hbm,
    drift_hbm,
    terminal_hbm,
    ex1_hbm,
    ex0_hbm,
    flags_hbm,
    v1_hbm,
    v0_hbm,
    precision_ref,
    drift_ref,
    flags_ref,
    nz_ref,
    n1_ref,
    n2_ref,
    terminal_ref,
    ex1_ref,
    ex0_ref,
    v1_ref,
    v0_ref,
    q1t,
    q1,
    t1,
    q0,
    t2,
    e1,
    e0,
    w0,
    st1,
    st0,
    f1,
    f0,
    price,
    out1,
    in1,
    out0,
    in0,
    q_send,
    q_recv,
    t_send,
    t_recv,
    s1_send,
    s1_recv,
    s0_send,
    s0_recv,
    p_send,
    p_recv,
    r1_send,
    r1_recv,
    r0_send,
    r0_recv,
    local,
):
    r = lax.axis_index("row")
    c = lax.axis_index("col")
    depth, own = n1_ref.shape
    sources = nz_ref.shape[1]
    lanes = q0.shape[1]
    height = q1t.shape[1]
    chunks, _, width = e1.shape
    barrier = pltpu.get_barrier_semaphore()
    for d in range(1, rows):
        pl.semaphore_signal(barrier, inc=1, device_id=(lax.rem(r + d, rows), c), device_id_type=MESH)
    for d in range(1, cols):
        pl.semaphore_signal(barrier, inc=1, device_id=(r, lax.rem(c + d, cols)), device_id_type=MESH)

    loads = [
        pltpu.make_async_copy(a, b, local.at[i])
        for i, (a, b) in enumerate(
            [
                (n1_hbm, n1_ref),
                (n2_hbm, n2_ref),
                (nz_hbm, nz_ref),
                (terminal_hbm, terminal_ref),
                (ex1_hbm, ex1_ref),
                (ex0_hbm, ex0_ref),
                (flags_hbm, flags_ref),
                (precision_hbm, precision_ref),
                (drift_hbm, drift_ref),
            ]
        )
    ]
    for load in loads[7:] + loads[:7]:
        load.start()
    loads[7].wait()
    loads[8].wait()
    precision = column_of(precision_ref[...])
    drift = column_of(drift_ref[...])
    loads[0].wait()
    mine = queries_of(n1_ref[...], precision, drift, height)
    q1t[c] = mine.astype(jnp.bfloat16)
    t1[r, :depth, :] = n1_ref[...].astype(jnp.bfloat16)
    for i in range(rows):
        t1[i, depth:, :] = ones_under(lanes - depth, own)
    loads[1].wait()
    for k in range(chunks):
        t2[k, :depth, :] = n2_ref[:, k * width : (k + 1) * width].astype(jnp.bfloat16)
        t2[k, depth:, :] = ones_under(lanes - depth, width)
    q1[c] = upright(mine, lanes)
    pl.semaphore_wait(barrier, rows + cols - 2)

    def to_rows(buf, send, recv):
        def make(d, slot):
            view = buf.at[slot, pl.ds(0, depth)] if buf is t1 else buf.at[slot]
            return pltpu.make_async_remote_copy(
                src_ref=view,
                dst_ref=view,
                send_sem=send.at[d],
                recv_sem=recv.at[d],
                device_id=(lax.rem(r + d, rows), c),
                device_id_type=MESH,
            )

        return make

    def start_rows(buf, send, recv):
        make = to_rows(buf, send, recv)
        for d in range(1, rows):
            make(d, r).start()

    def recv_rows(buf, send, recv):
        make = to_rows(buf, send, recv)
        for d in range(1, rows):
            make(d, lax.rem(r + rows - d, rows)).wait_recv()

    def sent_rows(buf, send, recv):
        make = to_rows(buf, send, recv)
        for d in range(1, rows):
            make(d, r).wait_send()

    def q_copy(d, slot):
        return pltpu.make_async_remote_copy(
            src_ref=q1t.at[slot],
            dst_ref=q1t.at[slot],
            send_sem=q_send.at[d],
            recv_sem=q_recv.at[d],
            device_id=(r, lax.rem(c + d, cols)),
            device_id_type=MESH,
        )

    for d in range(1, cols):
        q_copy(d, c).start()
    start_rows(t1, t_send, t_recv)

    loads[2].wait()
    q0[...] = upright(queries_of(nz_ref[...], precision, drift, height), lanes)
    step = min(TILE, sources)

    def stats(load_queries, load_targets, e, st, begin, end):
        def one(k, carry):
            target = load_targets(k)
            peak = None
            for at in range(0, sources, step):
                s = lax.dot_general(
                    load_queries(at), target, (((1,), (0,)), ((), ())), preferred_element_type=jnp.float32
                )
                e[k, at : at + step, :] = s
                top = jnp.max(s.reshape(step // 8, 8, width), axis=0)
                peak = top if peak is None else jnp.maximum(peak, top)
            peak = jnp.max(peak, axis=0, keepdims=True)
            total = jnp.zeros((8, width), jnp.float32)
            for at in range(0, sources, step):
                x = jnp.exp(e[k, at : at + step, :] - peak)
                e[k, at : at + step, :] = x
                total = total + jnp.sum(x.reshape(step // 8, 8, width), axis=0)
            st[r, 0, pl.ds(k, 1), :] = peak
            st[r, 1, pl.ds(k, 1), :] = jnp.sum(total, axis=0, keepdims=True)
            return carry

        lax.fori_loop(begin, end, one, 0)

    def factor(st, f):
        peak = st[0, 0]
        for i in range(1, rows):
            peak = jnp.maximum(peak, st[i, 0])
        total = jnp.zeros_like(peak)
        for i in range(rows):
            total = total + st[i, 1] * jnp.exp(st[i, 0] - peak)
        f[...] = jnp.exp(st[r, 0] - peak) * (1.0 / total)

    for d in range(1, cols):
        slot = lax.rem(c + cols - d, cols)
        q_copy(d, slot).wait_recv()
        q1[slot] = upright(q1t[slot].astype(jnp.float32), lanes)

    def q1_rows(at):
        return q1[at // own : (at + step) // own].reshape(step, q1.shape[2])

    stats(q1_rows, lambda k: t2[k], e1, st1, 0, chunks)
    start_rows(st1, s1_send, s1_recv)

    recv_rows(t1, t_send, t_recv)
    per = width // own

    def t1_rows(k):
        if per == 1:
            return t1[k]
        return jnp.concatenate([t1[k * per + i] for i in range(per)], axis=1)

    def stats_zero(begin, end):
        stats(lambda at: q0[at : at + step, :], t1_rows, e0, st0, begin, end)

    half = (chunks + 1) // 2
    stats_zero(0, half)

    recv_rows(st1, s1_send, s1_recv)
    factor(st1, f1)

    def partial_of(weights, load_prices, first, count):
        total = jnp.zeros((count, v1_ref.shape[1]), jnp.float32)
        for k in range(chunks):
            total = total + jnp.dot(weights(k, first, count), load_prices(k), preferred_element_type=jnp.float32)
        return total

    def carry_copy(out, into, send, recv, d, h, count):
        return pltpu.make_async_remote_copy(
            src_ref=out.at[d, pl.ds(h * count, count)],
            dst_ref=into.at[d, pl.ds(h * count, count)],
            send_sem=send.at[h * cols + d],
            recv_sem=recv.at[h * cols + d],
            device_id=(r, lax.rem(c + d, cols)),
            device_id_type=MESH,
        )

    def send_carry(weights, load_prices, out, into, send, recv, parts):
        count = own // parts
        for h in range(parts):
            for d in range(1, cols):
                first = lax.rem(c + d, cols) * own + h * count
                part = partial_of(weights, load_prices, first, count)
                out[d, h * count : (h + 1) * count, :] = part.astype(out.dtype)
                carry_copy(out, into, send, recv, d, h, count).start()
        return partial_of(weights, load_prices, c * own, own)

    def take_carry(total, out, into, send, recv, parts, h):
        count = own // parts
        piece = slice(h * count, (h + 1) * count)
        total = total[piece]
        for d in range(1, cols):
            carry_copy(out, into, send, recv, d, h, count).wait_recv()
            total = total + into[d, piece, :].astype(jnp.float32)
        return total

    def end_carry(out, into, send, recv, parts):
        for h in range(parts):
            for d in range(1, cols):
                carry_copy(out, into, send, recv, d, h, own // parts).wait_send()

    def weights_one(k, first, count):
        return (e1[k, pl.ds(first, count), :] * f1[pl.ds(k, 1), :]).astype(jnp.bfloat16)

    loads[3].wait()
    one = (out1, in1, r1_send, r1_recv, PARTS)
    held = send_carry(weights_one, lambda k: terminal_ref[k * width : (k + 1) * width, :], *one)
    stats_zero(half, chunks)
    start_rows(st0, s0_send, s0_recv)
    loads[4].wait()
    loads[6].wait()
    partner = r + 1 - 2 * lax.rem(r, 2)
    half_rows = rows // 2

    size = own // PARTS

    def along(k, h, slot):
        view = price.at[slot, pl.ds(h * size, size)]
        return pltpu.make_async_remote_copy(
            src_ref=view,
            dst_ref=view,
            send_sem=p_send.at[h * rows + k],
            recv_sem=p_recv.at[h * rows + k],
            device_id=(lax.rem(r + 2 * k, rows), c),
            device_id_type=MESH,
        )

    def across(k, h, slot):
        view = price.at[slot, pl.ds(h * size, size)]
        return pltpu.make_async_remote_copy(
            src_ref=view,
            dst_ref=view,
            send_sem=p_send.at[h * rows + half_rows + k],
            recv_sem=p_recv.at[h * rows + half_rows + k],
            device_id=(partner, c),
            device_id_type=MESH,
        )

    for h in range(PARTS):
        piece = slice(h * size, (h + 1) * size)
        carried = take_carry(held, *one, h)
        value = jnp.where(flags_ref[1:2, :] == 1, jnp.maximum(ex1_ref[piece, :], carried), carried)
        v1_ref[piece, :] = value
        price[r, piece, :] = value.astype(jnp.bfloat16)
        for k in range(1, half_rows):
            along(k, h, r).start()
        across(0, h, r).start()
    keep_one = pltpu.make_async_copy(v1_ref, v1_hbm, local.at[9])
    keep_one.start()

    recv_rows(st0, s0_send, s0_recv)
    factor(st0, f0)

    def weigh(k, carry):
        for at in range(0, sources, step):
            w0[k, at : at + step, :] = (e0[k, at : at + step, :] * f0[pl.ds(k, 1), :]).astype(jnp.bfloat16)
        return carry

    lax.fori_loop(0, chunks, weigh, 0)
    for h in range(PARTS):
        for k in range(1, half_rows):
            slot = lax.rem(r + rows - 2 * k, rows)
            along(k, h, slot).wait_recv()
            across(k, h, slot).start()
    for h in range(PARTS):
        for k in range(half_rows):
            across(k, h, lax.rem(partner + rows - 2 * k, rows)).wait_recv()

    def price_rows(k):
        return price[k * per : (k + 1) * per].reshape(width, price.shape[2])

    def weights_zero(k, first, count):
        return w0[k, pl.ds(first, count), :]

    zero = (out0, in0, r0_send, r0_recv, 1)
    held = send_carry(weights_zero, price_rows, *zero)
    loads[5].wait()
    carried = take_carry(held, *zero, 0)
    v0_ref[...] = jnp.where(flags_ref[0:1, :] == 1, jnp.maximum(ex0_ref[...], carried), carried)
    keep_zero = pltpu.make_async_copy(v0_ref, v0_hbm, local.at[10])
    keep_zero.start()

    for d in range(1, cols):
        q_copy(d, c).wait_send()
    sent_rows(t1, t_send, t_recv)
    sent_rows(st1, s1_send, s1_recv)
    sent_rows(st0, s0_send, s0_recv)
    for h in range(PARTS):
        for k in range(half_rows):
            across(k, h, r).wait_send()
            if k:
                along(k, h, r).wait_send()
    end_carry(*one)
    end_carry(*zero)
    keep_one.wait()
    keep_zero.wait()


def shards(rows, cols, nodes_zero, nodes_one, nodes_two, precision, drift, terminal, ex1, ex0, flags):
    own, depth = nodes_one.shape
    height = depth + 16
    sources = nodes_zero.shape[0]
    targets = nodes_two.shape[0]
    trades = terminal.shape[1]
    width = max(own, min(TILE, targets))
    chunks = targets // width
    lanes = 128 * (-(-(depth + 3) // 128))
    dma = pltpu.SemaphoreType.DMA
    out = jax.ShapeDtypeStruct((own, trades), jnp.float32)
    stat = pltpu.VMEM((rows, 2, chunks, width), jnp.float32)
    tall = pltpu.VMEM((chunks, sources, width), jnp.float32)
    few = pltpu.VMEM((chunks, width), jnp.float32)
    parts = pltpu.VMEM((cols, own, trades), jnp.float32)
    slim = pltpu.VMEM((cols, own, trades), jnp.bfloat16)
    anywhere = pl.BlockSpec(memory_space=pl.ANY)
    mine = pltpu.VMEM((own, trades), jnp.float32)
    return pl.pallas_call(
        functools.partial(body, rows, cols),
        out_shape=(out, out),
        in_specs=[pl.BlockSpec(memory_space=pltpu.HBM)] * 9,
        out_specs=(anywhere, anywhere),
        scratch_shapes=[
            pltpu.VMEM((1, depth), jnp.float32),
            pltpu.VMEM((1, depth), jnp.float32),
            pltpu.VMEM((2, trades), jnp.int32),
            pltpu.VMEM((depth, sources), jnp.float32),
            pltpu.VMEM((depth, own), jnp.float32),
            pltpu.VMEM((depth, targets), jnp.float32),
            pltpu.VMEM((targets, trades), jnp.bfloat16),
            mine,
            mine,
            mine,
            mine,
            pltpu.VMEM((cols, height, own), jnp.bfloat16),
            pltpu.VMEM((cols, own, lanes), jnp.bfloat16),
            pltpu.VMEM((rows, lanes, own), jnp.bfloat16),
            pltpu.VMEM((sources, lanes), jnp.bfloat16),
            pltpu.VMEM((chunks, lanes, width), jnp.bfloat16),
            tall,
            tall,
            pltpu.VMEM((chunks, sources, width), jnp.bfloat16),
            stat,
            stat,
            few,
            few,
            pltpu.VMEM((rows, own, trades), jnp.bfloat16),
            parts,
            parts,
            slim,
            slim,
            *[dma((cols,))] * 2,
            *[dma((rows,))] * 6,
            *[dma((PARTS * rows,))] * 2,
            *[dma((PARTS * cols,))] * 2,
            *[dma((cols,))] * 2,
            dma((11,)),
        ],
        compiler_params=pltpu.CompilerParams(
            collective_id=0, has_side_effects=True, vmem_limit_bytes=LIMIT
        ),
    )(nodes_zero.T, nodes_one.T, nodes_two.T, precision[None, :], drift[None, :], terminal, ex1, ex0, flags)


def solution(mesh):
    both = P(("row", "col"), None)
    return jax.shard_map(
        functools.partial(shards, mesh.shape["row"], mesh.shape["col"]),
        mesh=mesh,
        in_specs=(P("row", None), both, P("col", None), P(), P(), P("col", None), both, both, P()),
        out_specs=(both, both),
        check_vma=False,
    )
```
